512 devices in a mesh: segment: 2 (over x_hi), tile: 32 (over x_lo, z), stream: 8 (over y, core).
Axes of the slice: x: 4 (x_hi: 2, x_lo: 2; x = x_hi * 2 + x_lo), y: 4, z: 16, core: 2. Of those that a mesh axis runs over, the one named last changes fastest.
Arguments:
- frames: bfloat16 [8, 16, 2048, 256], P(None, 'stream', 'tile'), parts along dimension 1, may hold values from -6 to 6
- spatial_weight: bfloat16 [2, 2, 2304, 256], P('segment'), may hold values from -0.125 to 0.125
- temporal_weight: bfloat16 [2, 2, 768, 256], P('segment'), may hold values from -0.21875 to 0.21875
- ramp: int32 [32, 96], P('tile'), may hold values from 1 to 16
- intersection: int32 [32, 2], P('tile'), may hold values from 1 to 16, as said below
Outputs:
- encoded: bfloat16 [8, 16, 2048, 256], P('segment', 'stream', 'tile'), parts along dimension 1
The draws below stay inside these ranges and needn't reach their ends.
There are 8 independent parts, one for each index of `stream`. The reference program is written for one: setup_inputs(seed, part) draws one part's arguments, and reference() takes and returns one part's arrays. A program takes and returns all parts, laid end to end along the dimension named above; an argument that names none is the same for every part. Nothing has to cross between parts.
Inputs may be any that keep to these rules, and one draw needn't show every extreme that they name: `intersection`: each tile's two widths lie in 1 to 16; some tile has both equal to 16.
All inputs are finite; a program needn't handle non-finite values.
Results may differ from the reference program's by a relative error of at most 0.014.
Values may be sent and summed in bfloat16 or wider, within the bound.
A program may use at most 64 MiB of HBM per device.

```python
import jax
import jax.numpy as jnp
from jax import lax

C = 256
GROUPS = 32
FRAMES = 8
ROWS = 2
W_DEV = 64
MARGIN = 16
TILES = 32
SECTIONS = 2
W_EXT = 96
WIDTH = 2048


def draw_intersection(key, part):
    widths = jax.random.randint(jax.random.fold_in(key, 11), (TILES, 2), 1, MARGIN + 1)
    chosen = jax.random.randint(jax.random.fold_in(key, 12), (), 0, TILES)
    tile_rows = jnp.arange(TILES)[:, None]
    return jnp.where(tile_rows == chosen, MARGIN, widths).astype(jnp.int32)


def touch_ends(entries, key, smallest, top_value):
    extent = entries.shape
    spot = [jax.random.randint(jax.random.fold_in(key, axis), (), 0, extent[axis]) for axis in range(len(extent))]
    entries = entries.at[tuple(spot)].set(smallest)
    longest = extent.index(max(extent))
    spot[longest] = (spot[longest] + 1) % extent[longest]
    return entries.at[tuple(spot)].set(top_value)


def levels(rng, shape, split, low, largest):
    factor_of, own = 1.0, jax.random.fold_in(rng, 6)
    for dim, shards_of in split:
        heights = jnp.exp(jax.random.uniform(jax.random.fold_in(own, dim), (shards_of,), jnp.float32, low / len(split), largest / len(split)))
        factor_of = factor_of * jnp.repeat(heights, shape[dim] // shards_of).reshape([-1 if axis == dim else 1 for axis in range(len(shape))])
    return factor_of


def noise(rng, dims, scale, reach, shards=(), kind=jnp.bfloat16):
    array = scale * jax.random.normal(rng, dims, jnp.float32)
    if shards:
        array = array * levels(rng, dims, shards, -0.22, 0.18)
    return jnp.clip(array, -reach, reach).astype(kind)


def setup_inputs(seed: int = 0, part: int = 0) -> dict:
    keys = jax.random.split(jax.random.key(seed), 6)
    part_splits = jax.random.split(jax.random.fold_in(keys[5], part), 6)
    frames = noise(part_splits[0], (FRAMES, ROWS, WIDTH, C), 1.0, 6.0, ((2, 32),))
    spatial_weight = noise(keys[1], (SECTIONS, 2, 9 * C, C), (9 * C) ** -0.5, 0.125, ((0, 2),))
    temporal_weight = noise(keys[2], (SECTIONS, 2, 3 * C, C), (3 * C) ** -0.5, 0.21875, ((0, 2),))
    ramp = touch_ends(jax.random.randint(keys[3], (TILES, W_EXT), 1, 17), jax.random.fold_in(keys[3], 1), 1, 16).astype(jnp.int32)
    intersection = draw_intersection(jax.random.fold_in(keys[5], 71), part)
    return {"frames": frames, "spatial_weight": spatial_weight, "temporal_weight": temporal_weight, "ramp": ramp, "intersection": intersection}


def norm_silu(hidden):
    channels = hidden.shape[-1]
    group_width = channels // GROUPS
    chan_mean = lax.optimization_barrier(jnp.mean(hidden, axis=(1, 2)))
    group_mean = jnp.repeat(lax.optimization_barrier(jnp.mean(chan_mean.reshape(-1, GROUPS, group_width), axis=2)), group_width, axis=1)
    centered = hidden - group_mean[:, None, None, :]
    chan_var = lax.optimization_barrier(jnp.mean(centered * centered, axis=(1, 2)))
    group_var = jnp.repeat(lax.optimization_barrier(jnp.mean(chan_var.reshape(-1, GROUPS, group_width), axis=2)), group_width, axis=1)
    return jax.nn.silu(centered * lax.rsqrt(group_var + 1e-06)[:, None, None, :])

def spatial_conv(activity, weight):
    frame_count, row_count, column_count, channels = activity.shape
    padded = jnp.pad(activity, ((0, 0), (1, 1), (1, 1), (0, 0)))
    pieces = [padded[:, shift_row:shift_row + row_count, shift_col:shift_col + column_count, :] for shift_row in range(3) for shift_col in range(3)]
    stacked = jnp.concatenate(pieces, axis=-1).reshape(-1, 9 * channels)
    product = jnp.dot(stacked, weight, preferred_element_type=jnp.float32)
    return product.reshape(frame_count, row_count, column_count, -1)

def temporal_conv(spatial_out, weight, prior):
    frame_count = spatial_out.shape[0]
    sequence = jnp.concatenate([prior, spatial_out], axis=0)
    stacked = jnp.concatenate([sequence[0:frame_count], sequence[1:frame_count + 1], sequence[2:frame_count + 2]], axis=-1)
    product = jnp.dot(stacked.reshape(-1, stacked.shape[-1]), weight, preferred_element_type=jnp.float32)
    return (product.reshape(spatial_out.shape), sequence[frame_count:])

def residual_block(block_in, spatial_weights, temporal_weights, priors):
    hidden = block_in.astype(jnp.float32)
    new_priors = []
    for conv_index in range(2):
        activity = norm_silu(hidden).astype(jnp.bfloat16)
        spatial_out = spatial_conv(activity, spatial_weights[conv_index]).astype(jnp.bfloat16)
        hidden, state = temporal_conv(spatial_out, temporal_weights[conv_index], priors[conv_index])
        new_priors.append(state)
    result = (block_in.astype(jnp.float32) + hidden).astype(jnp.bfloat16)
    return (result, jnp.stack(new_priors))

def encode_tile(window, spatial_weight, temporal_weight):
    current = window
    for section_index in range(SECTIONS):
        priors = jnp.zeros((2, 2) + window.shape[1:], jnp.bfloat16)
        current, unused = residual_block(current, spatial_weight[section_index], temporal_weight[section_index], priors)
    return current

def reference(frames, spatial_weight, temporal_weight, ramp, intersection):
    padded = jnp.pad(frames, ((0, 0), (0, 0), (MARGIN, MARGIN), (0, 0)))
    starts = (jnp.arange(TILES) * W_DEV).astype(jnp.int32)

    def one_tile(start):
        window = lax.dynamic_slice_in_dim(padded, start, W_EXT, 2)
        return encode_tile(window, spatial_weight, temporal_weight)
    latents = lax.map(one_tile, starts)
    positions = jnp.arange(W_EXT)
    inside = (positions[None, :] >= MARGIN - intersection[:, :1]) & (positions[None, :] < MARGIN + W_DEV + intersection[:, 1:])
    weights = jnp.where(inside, ramp.astype(jnp.float32), 0.0)
    terms = latents.astype(jnp.float32) * weights[:, None, None, :, None]
    numer = terms[:, :, :, MARGIN:MARGIN + W_DEV, :]
    denom = weights[:, MARGIN:MARGIN + W_DEV]
    from_left = terms[:-1, :, :, MARGIN + W_DEV:, :]
    numer = numer + jnp.pad(from_left, ((1, 0), (0, 0), (0, 0), (0, W_DEV - MARGIN), (0, 0)))
    denom = denom + jnp.pad(weights[:-1, MARGIN + W_DEV:], ((1, 0), (0, W_DEV - MARGIN)))
    from_right = terms[1:, :, :, :MARGIN, :]
    numer = numer + jnp.pad(from_right, ((0, 1), (0, 0), (0, 0), (W_DEV - MARGIN, 0), (0, 0)))
    denom = denom + jnp.pad(weights[1:, :MARGIN], ((0, 1), (W_DEV - MARGIN, 0)))
    blended = (numer / denom[:, None, None, :, None]).astype(jnp.bfloat16)
    blended = jnp.transpose(blended, (1, 2, 0, 3, 4))
    return blended.reshape(FRAMES, ROWS, TILES * W_DEV, blended.shape[-1])
```

```python
import functools

import jax
import jax.numpy as jnp
from jax import lax
from jax.experimental import pallas as pl
from jax.experimental.pallas import tpu as pltpu
from jax.sharding import PartitionSpec as P

MARGIN = 16
LANES = 128
GROUP = 2
EPSILON = 1e-6
MESH = pl.DeviceIdType.MESH


def norm_act(hbuf, sbuf):
    frames, rows, columns, channels = hbuf.shape
    count = rows * columns
    halves = channels // LANES
    row8 = lax.broadcasted_iota(jnp.int32, (8, LANES), 0)
    lane8 = lax.broadcasted_iota(jnp.int32, (8, LANES), 1)
    means = jnp.zeros((8, LANES), jnp.float32)
    squares = jnp.zeros((8, LANES), jnp.float32)
    for f in range(frames):
        for h in range(halves):
            x = hbuf[f, :, :, h * LANES : (h + 1) * LANES].reshape(count, LANES)
            mean = jnp.sum(x, axis=0, keepdims=True) * (1.0 / count)
            d = x - mean
            square = jnp.sum(d * d, axis=0, keepdims=True)
            here = row8 == f * halves + h
            means = jnp.where(here, mean, means)
            squares = jnp.where(here, square, squares)
    size = float(count)
    for step in (1, 2, 4):
        low = (lane8 & step) == 0
        mean2 = jnp.where(low, pltpu.roll(means, LANES - step, 1), pltpu.roll(means, step, 1))
        square2 = jnp.where(low, pltpu.roll(squares, LANES - step, 1), pltpu.roll(squares, step, 1))
        d = means - mean2
        squares = squares + square2 + d * d * (0.5 * size)
        means = (means + mean2) * 0.5
        size = 2.0 * size
    scale = lax.rsqrt(squares * (1.0 / size) + EPSILON)
    column = lax.broadcasted_iota(jnp.int32, (columns, LANES), 0)
    for f in range(frames):
        for h in range(halves):
            at = f * halves + h
            mean = means[at : at + 1, :]
            inv = scale[at : at + 1, :]
            for r in range(rows):
                y = (hbuf[f, r, :, h * LANES : (h + 1) * LANES] - mean) * inv
                half = 0.5 * y
                a = half * jnp.tanh(half) + half
                before = jnp.where(column == 0, 0.0, pltpu.roll(a, 1, 0))
                after = jnp.where(column == columns - 1, 0.0, pltpu.roll(a, columns - 1, 0))
                for b, piece in enumerate((before, a, after)):
                    lane = (r * 3 + b) * channels + h * LANES
                    sbuf[f * columns : (f + 1) * columns, lane : lane + LANES] = piece.astype(jnp.bfloat16)


def kernel(
    tiles, frames, sw_hbm, tw_hbm, ramp, inter, out,
    xbuf, obuf, spat, hbuf, sbuf, sw, tw, wown, wtile, wleft, wright, mleft, mright, bbuf,
    own_sem, load_sem, halo_send, halo_recv, fwd_send, fwd_recv,
    wt_send, wt_recv, mg_send, mg_recv, ret_send, ret_recv,
):
    seg = lax.axis_index("segment")
    place = lax.axis_index("tile")
    stream = lax.axis_index("stream")
    total, rows, columns, channels = xbuf.shape
    owned = columns - 2 * MARGIN
    groups = total // GROUP
    half = groups // 2
    far = lax.rem(place + tiles // 2, tiles)
    left = lax.rem(place + tiles - 1, tiles)
    right = lax.rem(place + 1, tiles)
    tile = jnp.where(seg == 0, place, far)
    first, last = seg == 0, seg == 1

    def loads(k):
        return (
            pltpu.make_async_copy(sw_hbm.at[0, k], sw.at[k], load_sem.at[2 * k]),
            pltpu.make_async_copy(tw_hbm.at[0, k], tw.at[k], load_sem.at[2 * k + 1]),
        )

    def own(g):
        at = pl.ds(g * GROUP, GROUP)
        return pltpu.make_async_copy(
            frames.at[at], xbuf.at[at, :, MARGIN : MARGIN + owned, :], own_sem.at[g]
        )

    def remote(src, dst, send, recv, where):
        return pltpu.make_async_remote_copy(
            src_ref=src, dst_ref=dst, send_sem=send, recv_sem=recv, device_id=where, device_id_type=MESH
        )

    def halos(g):
        at = pl.ds(g * GROUP, GROUP)
        return (
            remote(
                frames.at[at, :, owned - MARGIN : owned, :], xbuf.at[at, :, 0:MARGIN, :],
                halo_send.at[0, g], halo_recv.at[0, g], (seg, right, stream),
            ),
            remote(
                frames.at[at, :, 0:MARGIN, :], xbuf.at[at, :, MARGIN + owned : columns, :],
                halo_send.at[1, g], halo_recv.at[1, g], (seg, left, stream),
            ),
        )

    def forward(g):
        at = pl.ds(g * GROUP, GROUP)
        return remote(obuf.at[at], xbuf.at[at], fwd_send.at[g], fwd_recv.at[g], (1 - seg, far, stream))

    def weight_over():
        return remote(wown, wtile, wt_send.at[0], wt_recv.at[0], (1 - seg, far, stream))

    def weight_sides():
        return (
            remote(wtile.at[0:MARGIN], wright, wt_send.at[1], wt_recv.at[1], (seg, left, stream)),
            remote(wtile.at[columns - MARGIN : columns], wleft, wt_send.at[2], wt_recv.at[2], (seg, right, stream)),
        )

    def margins(g):
        at = pl.ds(g * GROUP, GROUP)
        return (
            remote(
                obuf.at[at, :, 0:MARGIN, :], mright.at[at],
                mg_send.at[0, g], mg_recv.at[0, g], (seg, left, stream),
            ),
            remote(
                obuf.at[at, :, columns - MARGIN : columns, :], mleft.at[at],
                mg_send.at[1, g], mg_recv.at[1, g], (seg, right, stream),
            ),
        )

    def give(g):
        to = g // half
        place_in = g % half
        return remote(
            bbuf.at[pl.ds(g * GROUP, GROUP)], out.at[pl.ds(place_in * GROUP, GROUP)],
            ret_send.at[g], ret_recv.at[place_in], (to, far, stream),
        )

    for k in range(2):
        for copy in loads(k):
            copy.start()

    @pl.when(first)
    def _():
        for g in range(groups):
            own(g).start()

    barrier = pltpu.get_barrier_semaphore()
    for where in ((seg, left, stream), (seg, right, stream), (1 - seg, far, stream)):
        pl.semaphore_signal(barrier, inc=1, device_id=where, device_id_type=MESH)

    @pl.when(last)
    def _():
        pl.semaphore_signal(barrier, inc=1, device_id=(seg, far, stream), device_id_type=MESH)

    pl.semaphore_wait(barrier, 3 + seg)

    @pl.when(first)
    def _():
        for g in range(groups):
            for copy in halos(g):
                copy.start()
        eye = lax.broadcasted_iota(jnp.int32, (columns, columns), 0) == lax.broadcasted_iota(
            jnp.int32, (columns, columns), 1
        )
        spread = jnp.where(eye, ramp[...].astype(jnp.float32), 0.0)
        weight = jnp.broadcast_to(jnp.sum(spread, axis=1, keepdims=True), (columns, LANES))
        position = lax.broadcasted_iota(jnp.int32, (columns, LANES), 0)
        inside = (position >= MARGIN - inter[0, 0]) & (position < MARGIN + owned + inter[0, 1])
        wown[...] = jnp.where(inside, weight, 0.0).astype(jnp.bfloat16)
        weight_over().start()

    for k in range(2):
        spat[k, 0:2] = jnp.zeros((2, rows, columns, channels), jnp.bfloat16)

    @pl.when(last)
    def _():
        weight_over().wait_recv()
        for copy in weight_sides():
            copy.start()

    def conv(k, g):
        norm_act(hbuf, sbuf)
        taps = 2 * 3 * channels
        act = sbuf[...]
        for r in range(rows):
            low = (1 - r) * 3 * channels
            product = jnp.dot(act, sw[k, low : low + taps, :], preferred_element_type=jnp.float32)
            spat[k, pl.ds(g * GROUP + 2, GROUP), r] = product.reshape(GROUP, columns, channels).astype(jnp.bfloat16)
        pieces = [
            spat[k, pl.ds(g * GROUP + q, GROUP)].reshape(GROUP * rows * columns, channels) for q in range(3)
        ]
        product = jnp.dot(jnp.concatenate(pieces, axis=-1), tw[k], preferred_element_type=jnp.float32)
        return product.reshape(GROUP, rows, columns, channels)

    def blend(g):
        for copy in margins(g):
            copy.wait_recv()
        own_w = wtile[MARGIN : MARGIN + owned, :].astype(jnp.float32)
        left_w = wleft[...].astype(jnp.float32) * (tile > 0).astype(jnp.float32)
        right_w = wright[...].astype(jnp.float32) * (tile < tiles - 1).astype(jnp.float32)
        parts = ((0, MARGIN, left_w, mleft), (MARGIN, owned - MARGIN, None, None), (owned - MARGIN, owned, right_w, mright))
        for low, high, side_w, side in parts:
            w = own_w[low:high]
            inv = 1.0 / (w if side is None else w + side_w)
            for f in range(GROUP):
                frame = g * GROUP + f
                for r in range(rows):
                    for h in range(channels // LANES):
                        lanes = slice(h * LANES, (h + 1) * LANES)
                        total_term = obuf[frame, r, MARGIN + low : MARGIN + high, lanes].astype(jnp.float32) * w
                        if side is not None:
                            total_term = total_term + side[frame, r, :, lanes].astype(jnp.float32) * side_w
                        bbuf[frame, r, low:high, lanes] = (total_term * inv).astype(jnp.bfloat16)
        give(g).start()

    def step(g):
        at = pl.ds(g * GROUP, GROUP)

        @pl.when(first)
        def _():
            own(g).wait()
            for copy in halos(g):
                copy.wait_recv()

            @pl.when(tile == 0)
            def _():
                xbuf[at, :, 0:MARGIN, :] = jnp.zeros((GROUP, rows, MARGIN, channels), jnp.bfloat16)

            @pl.when(tile == tiles - 1)
            def _():
                xbuf[at, :, MARGIN + owned : columns, :] = jnp.zeros((GROUP, rows, MARGIN, channels), jnp.bfloat16)

        @pl.when(last)
        def _():
            forward(g).wait_recv()

        hbuf[...] = xbuf[at].astype(jnp.float32)

        if g == 0:
            for copy in loads(0):
                copy.wait()

        hbuf[...] = conv(0, g)

        if g == 0:
            for copy in loads(1):
                copy.wait()

        obuf[at] = (xbuf[at].astype(jnp.float32) + conv(1, g)).astype(jnp.bfloat16)

        @pl.when(first)
        def _():
            forward(g).start()

        @pl.when(last)
        def _():
            for copy in margins(g):
                copy.start()

            if g == 0:
                for copy in weight_sides():
                    copy.wait_recv()
            else:
                blend(g - 1)

    for g in range(groups):
        step(g)

    @pl.when(last)
    def _():
        blend(groups - 1)
        for copy in weight_sides():
            copy.wait_send()
        for g in range(groups):
            for copy in margins(g):
                copy.wait_send()
            give(g).wait_send()

    @pl.when(first)
    def _():
        weight_over().wait_send()
        for g in range(groups):
            for copy in halos(g):
                copy.wait_send()
            forward(g).wait_send()

    for g in range(half):
        give(g).wait_recv()


def body(tiles, frames, spatial_weight, temporal_weight, ramp, intersection):
    total, rows, owned, channels = frames.shape
    columns = owned + 2 * MARGIN
    groups = total // GROUP
    bf16, f32 = jnp.bfloat16, jnp.float32
    dma = pltpu.SemaphoreType.DMA
    return pl.pallas_call(
        functools.partial(kernel, tiles),
        out_shape=jax.ShapeDtypeStruct((total // 2, rows, owned, channels), bf16),
        in_specs=[
            pl.BlockSpec(memory_space=pl.ANY),
            pl.BlockSpec(memory_space=pl.ANY),
            pl.BlockSpec(memory_space=pl.ANY),
            pl.BlockSpec(memory_space=pltpu.VMEM),
            pl.BlockSpec(memory_space=pltpu.SMEM),
        ],
        out_specs=pl.BlockSpec(memory_space=pl.ANY),
        scratch_shapes=[
            pltpu.VMEM((total, rows, columns, channels), bf16),
            pltpu.VMEM((total, rows, columns, channels), bf16),
            pltpu.VMEM((2, total + 2, rows, columns, channels), bf16),
            pltpu.VMEM((GROUP, rows, columns, channels), f32),
            pltpu.VMEM((GROUP * columns, rows * 3 * channels), bf16),
            pltpu.VMEM(spatial_weight.shape[1:], bf16),
            pltpu.VMEM(temporal_weight.shape[1:], bf16),
            pltpu.VMEM((columns, LANES), bf16),
            pltpu.VMEM((columns, LANES), bf16),
            pltpu.VMEM((MARGIN, LANES), bf16),
            pltpu.VMEM((MARGIN, LANES), bf16),
            pltpu.VMEM((total, rows, MARGIN, channels), bf16),
            pltpu.VMEM((total, rows, MARGIN, channels), bf16),
            pltpu.VMEM((total, rows, owned, channels), bf16),
            dma((groups,)),
            dma((4,)),
            dma((2, groups)),
            dma((2, groups)),
            dma((groups,)),
            dma((groups,)),
            dma((3,)),
            dma((3,)),
            dma((2, groups)),
            dma((2, groups)),
            dma((groups,)),
            dma((groups // 2,)),
        ],
        compiler_params=pltpu.CompilerParams(
            collective_id=0, has_side_effects=True, vmem_limit_bytes=48 * 1024 * 1024
        ),
    )(frames, spatial_weight, temporal_weight, ramp, intersection)


def solution(mesh):
    in_specs = (
        P(None, "stream", "tile", None),
        P("segment", None, None, None),
        P("segment", None, None, None),
        P("tile", None),
        P("tile", None),
    )
    out_specs = P("segment", "stream", "tile", None)
    return jax.shard_map(
        functools.partial(body, mesh.shape["tile"]),
        mesh=mesh, in_specs=in_specs, out_specs=out_specs, check_vma=False,
    )
```

```python
import functools

import jax
import jax.numpy as jnp
from jax import lax
from jax.experimental import pallas as pl
from jax.experimental.pallas import tpu as pltpu
from jax.sharding import PartitionSpec as P

MARGIN = 16
LANES = 128
GROUP = 2
EPSILON = 1e-6
MESH = pl.DeviceIdType.MESH


def norm_act(hbuf, sbuf):
    frames, rows, columns, channels = hbuf.shape
    count = rows * columns
    halves = channels // LANES
    row8 = lax.broadcasted_iota(jnp.int32, (8, LANES), 0)
    lane8 = lax.broadcasted_iota(jnp.int32, (8, LANES), 1)
    means = jnp.zeros((8, LANES), jnp.float32)
    squares = jnp.zeros((8, LANES), jnp.float32)
    for f in range(frames):
        for h in range(halves):
            x = hbuf[f, :, :, h * LANES : (h + 1) * LANES].reshape(count, LANES)
            mean = jnp.sum(x, axis=0, keepdims=True) * (1.0 / count)
            d = x - mean
            square = jnp.sum(d * d, axis=0, keepdims=True)
            here = row8 == f * halves + h
            means = jnp.where(here, mean, means)
            squares = jnp.where(here, square, squares)
    size = float(count)
    for step in (1, 2, 4):
        low = (lane8 & step) == 0
        mean2 = jnp.where(low, pltpu.roll(means, LANES - step, 1), pltpu.roll(means, step, 1))
        square2 = jnp.where(low, pltpu.roll(squares, LANES - step, 1), pltpu.roll(squares, step, 1))
        d = means - mean2
        squares = squares + square2 + d * d * (0.5 * size)
        means = (means + mean2) * 0.5
        size = 2.0 * size
    scale = lax.rsqrt(squares * (1.0 / size) + EPSILON)
    column = lax.broadcasted_iota(jnp.int32, (columns, LANES), 0)
    for f in range(frames):
        for h in range(halves):
            at = f * halves + h
            mean = means[at : at + 1, :]
            inv = scale[at : at + 1, :]
            for r in range(rows):
                y = (hbuf[f, r, :, h * LANES : (h + 1) * LANES] - mean) * inv
                half = 0.5 * y
                a = half * jnp.tanh(half) + half
                before = jnp.where(column == 0, 0.0, pltpu.roll(a, 1, 0))
                after = jnp.where(column == columns - 1, 0.0, pltpu.roll(a, columns - 1, 0))
                for b, piece in enumerate((before, a, after)):
                    lane = (r * 3 + b) * channels + h * LANES
                    sbuf[f * columns : (f + 1) * columns, lane : lane + LANES] = piece.astype(jnp.bfloat16)


def kernel(
    tiles, frames, sw_hbm, tw_hbm, ramp, inter, out,
    xbuf, obuf, spat, hbuf, sbuf, sw, tw, wown, wtile, wleft, wright, mleft, mright, bbuf,
    own_sem, load_sem, halo_send, halo_recv, fwd_send, fwd_recv,
    wt_send, wt_recv, mg_send, mg_recv, ret_send, ret_recv,
):
    seg = lax.axis_index("segment")
    place = lax.axis_index("tile")
    stream = lax.axis_index("stream")
    total, rows, columns, channels = xbuf.shape
    owned = columns - 2 * MARGIN
    groups = total // GROUP
    half = groups // 2
    far = lax.rem(place + tiles // 2, tiles)
    left = lax.rem(place + tiles - 1, tiles)
    right = lax.rem(place + 1, tiles)
    tile = jnp.where(seg == 0, place, far)
    first, last = seg == 0, seg == 1

    def loads(k):
        return (
            pltpu.make_async_copy(sw_hbm.at[0, k], sw.at[k], load_sem.at[2 * k]),
            pltpu.make_async_copy(tw_hbm.at[0, k], tw.at[k], load_sem.at[2 * k + 1]),
        )

    def own(g):
        at = pl.ds(g * GROUP, GROUP)
        return pltpu.make_async_copy(
            frames.at[at], xbuf.at[at, :, MARGIN : MARGIN + owned, :], own_sem.at[g]
        )

    def remote(src, dst, send, recv, where):
        return pltpu.make_async_remote_copy(
            src_ref=src, dst_ref=dst, send_sem=send, recv_sem=recv, device_id=where, device_id_type=MESH
        )

    def halos(g):
        at = pl.ds(g * GROUP, GROUP)
        return (
            remote(
                frames.at[at, :, owned - MARGIN : owned, :], xbuf.at[at, :, 0:MARGIN, :],
                halo_send.at[0, g], halo_recv.at[0, g], (seg, right, stream),
            ),
            remote(
                frames.at[at, :, 0:MARGIN, :], xbuf.at[at, :, MARGIN + owned : columns, :],
                halo_send.at[1, g], halo_recv.at[1, g], (seg, left, stream),
            ),
        )

    def forward(g):
        at = pl.ds(g * GROUP, GROUP)
        return remote(obuf.at[at], xbuf.at[at], fwd_send.at[g], fwd_recv.at[g], (1 - seg, far, stream))

    def weight_over():
        return remote(wown, wtile, wt_send.at[0], wt_recv.at[0], (1 - seg, far, stream))

    def weight_sides():
        return (
            remote(wtile.at[0:MARGIN], wright, wt_send.at[1], wt_recv.at[1], (seg, left, stream)),
            remote(wtile.at[columns - MARGIN : columns], wleft, wt_send.at[2], wt_recv.at[2], (seg, right, stream)),
        )

    def margins(g):
        at = pl.ds(g * GROUP, GROUP)
        return (
            remote(
                obuf.at[at, :, 0:MARGIN, :], mright.at[at],
                mg_send.at[0, g], mg_recv.at[0, g], (seg, left, stream),
            ),
            remote(
                obuf.at[at, :, columns - MARGIN : columns, :], mleft.at[at],
                mg_send.at[1, g], mg_recv.at[1, g], (seg, right, stream),
            ),
        )

    def give(g):
        to = g // half
        place_in = g % half
        return remote(
            bbuf.at[pl.ds(g * GROUP, GROUP)], out.at[pl.ds(place_in * GROUP, GROUP)],
            ret_send.at[g], ret_recv.at[place_in], (to, far, stream),
        )

    for k in range(2):
        for copy in loads(k):
            copy.start()

    @pl.when(first)
    def _():
        for g in range(groups):
            own(g).start()

    barrier = pltpu.get_barrier_semaphore()
    for where in ((seg, left, stream), (seg, right, stream), (1 - seg, far, stream)):
        pl.semaphore_signal(barrier, inc=1, device_id=where, device_id_type=MESH)

    @pl.when(last)
    def _():
        pl.semaphore_signal(barrier, inc=1, device_id=(seg, far, stream), device_id_type=MESH)

    pl.semaphore_wait(barrier, 3 + seg)

    @pl.when(first)
    def _():
        for g in range(groups):
            for copy in halos(g):
                copy.start()
        eye = lax.broadcasted_iota(jnp.int32, (columns, columns), 0) == lax.broadcasted_iota(
            jnp.int32, (columns, columns), 1
        )
        spread = jnp.where(eye, ramp[...].astype(jnp.float32), 0.0)
        weight = jnp.broadcast_to(jnp.sum(spread, axis=1, keepdims=True), (columns, LANES))
        position = lax.broadcasted_iota(jnp.int32, (columns, LANES), 0)
        inside = (position >= MARGIN - inter[0, 0]) & (position < MARGIN + owned + inter[0, 1])
        wown[...] = jnp.where(inside, weight, 0.0).astype(jnp.bfloat16)
        weight_over().start()

    for k in range(2):
        spat[k, 0:2] = jnp.zeros((2, rows, columns, channels), jnp.bfloat16)

    @pl.when(last)
    def _():
        weight_over().wait_recv()
        for copy in weight_sides():
            copy.start()

    def conv(k, g):
        norm_act(hbuf, sbuf)
        taps = 2 * 3 * channels
        act = sbuf[...]
        for r in range(rows):
            low = (1 - r) * 3 * channels
            product = jnp.dot(act, sw[k, low : low + taps, :], preferred_element_type=jnp.float32)
            spat[k, pl.ds(g * GROUP + 2, GROUP), r] = product.reshape(GROUP, columns, channels).astype(jnp.bfloat16)
        pieces = [
            spat[k, pl.ds(g * GROUP + q, GROUP)].reshape(GROUP * rows * columns, channels) for q in range(3)
        ]
        product = jnp.dot(jnp.concatenate(pieces, axis=-1), tw[k], preferred_element_type=jnp.float32)
        return product.reshape(GROUP, rows, columns, channels)

    def blend(g):
        for copy in margins(g):
            copy.wait_recv()
        own_w = wtile[MARGIN : MARGIN + owned, :].astype(jnp.float32)
        left_w = wleft[...].astype(jnp.float32) * (tile > 0).astype(jnp.float32)
        right_w = wright[...].astype(jnp.float32) * (tile < tiles - 1).astype(jnp.float32)
        parts = ((0, MARGIN, left_w, mleft), (MARGIN, owned - MARGIN, None, None), (owned - MARGIN, owned, right_w, mright))
        for low, high, side_w, side in parts:
            w = own_w[low:high]
            inv = 1.0 / (w if side is None else w + side_w)
            for f in range(GROUP):
                frame = g * GROUP + f
                for r in range(rows):
                    for h in range(channels // LANES):
                        lanes = slice(h * LANES, (h + 1) * LANES)
                        total_term = obuf[frame, r, MARGIN + low : MARGIN + high, lanes].astype(jnp.float32) * w
                        if side is not None:
                            total_term = total_term + side[frame, r, :, lanes].astype(jnp.float32) * side_w
                        bbuf[frame, r, low:high, lanes] = (total_term * inv).astype(jnp.bfloat16)
        give(g).start()

    def step(g):
        at = pl.ds(g * GROUP, GROUP)

        @pl.when(first)
        def _():
            own(g).wait()
            for copy in halos(g):
                copy.wait_recv()

            @pl.when(tile == 0)
            def _():
                xbuf[at, :, 0:MARGIN, :] = jnp.zeros((GROUP, rows, MARGIN, channels), jnp.bfloat16)

            @pl.when(tile == tiles - 1)
            def _():
                xbuf[at, :, MARGIN + owned : columns, :] = jnp.zeros((GROUP, rows, MARGIN, channels), jnp.bfloat16)

        @pl.when(last)
        def _():
            forward(g).wait_recv()

        hbuf[...] = xbuf[at].astype(jnp.float32)

        if g == 0:
            for copy in loads(0):
                copy.wait()

        hbuf[...] = conv(0, g)

        if g == 0:
            for copy in loads(1):
                copy.wait()

        obuf[at] = (xbuf[at].astype(jnp.float32) + conv(1, g)).astype(jnp.bfloat16)

        @pl.when(first)
        def _():
            forward(g).start()

        @pl.when(last)
        def _():
            for copy in margins(g):
                copy.start()

            if g == 0:
                for copy in weight_sides():
                    copy.wait_recv()
            else:
                blend(g - 1)

    for g in range(groups):
        step(g)

    @pl.when(last)
    def _():
        blend(groups - 1)
        for copy in weight_sides():
            copy.wait_send()
        for g in range(groups):
            for copy in margins(g):
                copy.wait_send()
            give(g).wait_send()

    @pl.when(first)
    def _():
        weight_over().wait_send()
        for g in range(groups):
            for copy in halos(g):
                copy.wait_send()
            forward(g).wait_send()

    for g in range(half):
        give(g).wait_recv()


def body(tiles, frames, spatial_weight, temporal_weight, ramp, intersection):
    total, rows, owned, channels = frames.shape
    columns = owned + 2 * MARGIN
    groups = total // GROUP
    bf16, f32 = jnp.bfloat16, jnp.float32
    dma = pltpu.SemaphoreType.DMA
    return pl.pallas_call(
        functools.partial(kernel, tiles),
        out_shape=jax.ShapeDtypeStruct((total // 2, rows, owned, channels), bf16),
        in_specs=[
            pl.BlockSpec(memory_space=pltpu.HBM),
            pl.BlockSpec(memory_space=pltpu.HBM),
            pl.BlockSpec(memory_space=pltpu.HBM),
            pl.BlockSpec(memory_space=pltpu.VMEM),
            pl.BlockSpec(memory_space=pltpu.SMEM),
        ],
        out_specs=pl.BlockSpec(memory_space=pltpu.HBM),
        scratch_shapes=[
            pltpu.VMEM((total, rows, columns, channels), bf16),
            pltpu.VMEM((total, rows, columns, channels), bf16),
            pltpu.VMEM((2, total + 2, rows, columns, channels), bf16),
            pltpu.VMEM((GROUP, rows, columns, channels), f32),
            pltpu.VMEM((GROUP * columns, rows * 3 * channels), bf16),
            pltpu.VMEM(spatial_weight.shape[1:], bf16),
            pltpu.VMEM(temporal_weight.shape[1:], bf16),
            pltpu.VMEM((columns, LANES), bf16),
            pltpu.VMEM((columns, LANES), bf16),
            pltpu.VMEM((MARGIN, LANES), bf16),
            pltpu.VMEM((MARGIN, LANES), bf16),
            pltpu.VMEM((total, rows, MARGIN, channels), bf16),
            pltpu.VMEM((total, rows, MARGIN, channels), bf16),
            pltpu.VMEM((total, rows, owned, channels), bf16),
            dma((groups,)),
            dma((4,)),
            dma((2, groups)),
            dma((2, groups)),
            dma((groups,)),
            dma((groups,)),
            dma((3,)),
            dma((3,)),
            dma((2, groups)),
            dma((2, groups)),
            dma((groups,)),
            dma((groups // 2,)),
        ],
        compiler_params=pltpu.CompilerParams(
            collective_id=0, has_side_effects=True, vmem_limit_bytes=60 * 1024 * 1024
        ),
    )(frames, spatial_weight, temporal_weight, ramp, intersection)


def solution(mesh):
    in_specs = (
        P(None, "stream", "tile", None),
        P("segment", None, None, None),
        P("segment", None, None, None),
        P("tile", None),
        P("tile", None),
    )
    out_specs = P("segment", "stream", "tile", None)
    return jax.shard_map(
        functools.partial(body, mesh.shape["tile"]),
        mesh=mesh, in_specs=in_specs, out_specs=out_specs, check_vma=False,
    )
```

```python
import functools

import jax
import jax.numpy as jnp
from jax import lax
from jax.experimental import pallas as pl
from jax.experimental.pallas import tpu as pltpu
from jax.sharding import PartitionSpec as P

MARGIN = 16
LANES = 128
GROUP = 1
EPSILON = 1e-6
MESH = pl.DeviceIdType.MESH


def norm_act(hbuf, sbuf):
    frames, rows, columns, channels = hbuf.shape
    count = rows * columns
    halves = channels // LANES
    row8 = lax.broadcasted_iota(jnp.int32, (8, LANES), 0)
    lane8 = lax.broadcasted_iota(jnp.int32, (8, LANES), 1)
    means = jnp.zeros((8, LANES), jnp.float32)
    squares = jnp.zeros((8, LANES), jnp.float32)
    for f in range(frames):
        for h in range(halves):
            x = hbuf[f, :, :, h * LANES : (h + 1) * LANES].reshape(count, LANES)
            mean = jnp.sum(x, axis=0, keepdims=True) * (1.0 / count)
            d = x - mean
            square = jnp.sum(d * d, axis=0, keepdims=True)
            here = row8 == f * halves + h
            means = jnp.where(here, mean, means)
            squares = jnp.where(here, square, squares)
    size = float(count)
    for step in (1, 2, 4):
        low = (lane8 & step) == 0
        mean2 = jnp.where(low, pltpu.roll(means, LANES - step, 1), pltpu.roll(means, step, 1))
        square2 = jnp.where(low, pltpu.roll(squares, LANES - step, 1), pltpu.roll(squares, step, 1))
        d = means - mean2
        squares = squares + square2 + d * d * (0.5 * size)
        means = (means + mean2) * 0.5
        size = 2.0 * size
    scale = lax.rsqrt(squares * (1.0 / size) + EPSILON)
    column = lax.broadcasted_iota(jnp.int32, (columns, LANES), 0)
    for f in range(frames):
        for h in range(halves):
            at = f * halves + h
            mean = means[at : at + 1, :]
            inv = scale[at : at + 1, :]
            for r in range(rows):
                y = (hbuf[f, r, :, h * LANES : (h + 1) * LANES] - mean) * inv
                half = 0.5 * y
                a = half * jnp.tanh(half) + half
                before = jnp.where(column == 0, 0.0, pltpu.roll(a, 1, 0))
                after = jnp.where(column == columns - 1, 0.0, pltpu.roll(a, columns - 1, 0))
                for b, piece in enumerate((before, a, after)):
                    lane = (r * 3 + b) * channels + h * LANES
                    sbuf[f * columns : (f + 1) * columns, lane : lane + LANES] = piece.astype(jnp.bfloat16)


def kernel(
    tiles, frames, sw_hbm, tw_hbm, ramp, inter, out,
    xbuf, obuf, spat, hbuf, sbuf, sw, tw, wtile, wleft, wright, mleft, mright, bbuf,
    own_sem, load_sem, halo_send, halo_recv, fwd_send, fwd_recv,
    wt_send, wt_recv, mg_send, mg_recv, ret_send, ret_recv,
):
    seg = lax.axis_index("segment")
    place = lax.axis_index("tile")
    stream = lax.axis_index("stream")
    total, rows, columns, channels = xbuf.shape
    owned = columns - 2 * MARGIN
    groups = total // GROUP
    half = groups // 2
    left = lax.rem(place + tiles - 1, tiles)
    right = lax.rem(place + 1, tiles)
    first, last = seg == 0, seg == 1

    def loads(k):
        return (
            pltpu.make_async_copy(sw_hbm.at[0, k], sw.at[k], load_sem.at[2 * k]),
            pltpu.make_async_copy(tw_hbm.at[0, k], tw.at[k], load_sem.at[2 * k + 1]),
        )

    def own(g):
        at = pl.ds(g * GROUP, GROUP)
        return pltpu.make_async_copy(
            frames.at[at], xbuf.at[at, :, MARGIN : MARGIN + owned, :], own_sem.at[g]
        )

    def remote(src, dst, send, recv, where):
        return pltpu.make_async_remote_copy(
            src_ref=src, dst_ref=dst, send_sem=send, recv_sem=recv, device_id=where, device_id_type=MESH
        )

    def halos(g):
        at = pl.ds(g * GROUP, GROUP)
        return (
            remote(
                frames.at[at, :, owned - MARGIN : owned, :], xbuf.at[at, :, 0:MARGIN, :],
                halo_send.at[0, g], halo_recv.at[0, g], (seg, right, stream),
            ),
            remote(
                frames.at[at, :, 0:MARGIN, :], xbuf.at[at, :, MARGIN + owned : columns, :],
                halo_send.at[1, g], halo_recv.at[1, g], (seg, left, stream),
            ),
        )

    def forward(g):
        at = pl.ds(g * GROUP, GROUP)
        return remote(obuf.at[at], xbuf.at[at], fwd_send.at[g], fwd_recv.at[g], (1 - seg, place, stream))

    def weight_sides():
        return (
            remote(wtile.at[0:MARGIN], wright, wt_send.at[0], wt_recv.at[0], (seg, left, stream)),
            remote(wtile.at[columns - MARGIN : columns], wleft, wt_send.at[1], wt_recv.at[1], (seg, right, stream)),
        )

    def margins(g):
        at = pl.ds(g * GROUP, GROUP)
        return (
            remote(
                obuf.at[at, :, 0:MARGIN, :], mright.at[at],
                mg_send.at[0, g], mg_recv.at[0, g], (seg, left, stream),
            ),
            remote(
                obuf.at[at, :, columns - MARGIN : columns, :], mleft.at[at],
                mg_send.at[1, g], mg_recv.at[1, g], (seg, right, stream),
            ),
        )

    def give(g):
        at = pl.ds(g % half * GROUP, GROUP)
        src = bbuf.at[pl.ds(g * GROUP, GROUP)]
        if g < half:
            return remote(src, out.at[at], ret_send.at[g], ret_recv.at[g], (1 - seg, place, stream))
        return pltpu.make_async_copy(src, out.at[at], ret_send.at[g])

    barrier = pltpu.get_barrier_semaphore()
    for where in ((seg, left, stream), (seg, right, stream), (1 - seg, place, stream)):
        pl.semaphore_signal(barrier, inc=1, device_id=where, device_id_type=MESH)

    @pl.when(first)
    def _():
        own(0).start()

    for copy in loads(0):
        copy.start()

    @pl.when(first)
    def _():
        for g in range(1, groups):
            own(g).start()

    for copy in loads(1):
        copy.start()

    pl.semaphore_wait(barrier, 3)

    @pl.when(first)
    def _():
        for g in range(groups):
            for copy in halos(g):
                copy.start()

    @pl.when(last)
    def _():
        eye = lax.broadcasted_iota(jnp.int32, (columns, columns), 0) == lax.broadcasted_iota(
            jnp.int32, (columns, columns), 1
        )
        spread = jnp.where(eye, ramp[...].astype(jnp.float32), 0.0)
        weight = jnp.broadcast_to(jnp.sum(spread, axis=1, keepdims=True), (columns, LANES))
        position = lax.broadcasted_iota(jnp.int32, (columns, LANES), 0)
        inside = (position >= MARGIN - inter[0, 0]) & (position < MARGIN + owned + inter[0, 1])
        wtile[...] = jnp.where(inside, weight, 0.0).astype(jnp.bfloat16)
        for copy in weight_sides():
            copy.start()

    for k in range(2):
        spat[k, 0:2] = jnp.zeros((2, rows, columns, channels), jnp.bfloat16)

    def conv(k, g):
        norm_act(hbuf, sbuf)
        taps = 2 * 3 * channels
        act = sbuf[...]
        for r in range(rows):
            low = (1 - r) * 3 * channels
            product = jnp.dot(act, sw[k, low : low + taps, :], preferred_element_type=jnp.float32)
            spat[k, pl.ds(g * GROUP + 2, GROUP), r] = product.reshape(GROUP, columns, channels).astype(jnp.bfloat16)
        pieces = [
            spat[k, pl.ds(g * GROUP + q, GROUP)].reshape(GROUP * rows * columns, channels) for q in range(3)
        ]
        product = jnp.dot(jnp.concatenate(pieces, axis=-1), tw[k], preferred_element_type=jnp.float32)
        return product.reshape(GROUP, rows, columns, channels)

    def blend(g):
        for copy in margins(g):
            copy.wait_recv()
        own_w = wtile[MARGIN : MARGIN + owned, :].astype(jnp.float32)
        left_w = wleft[...].astype(jnp.float32) * (place > 0).astype(jnp.float32)
        right_w = wright[...].astype(jnp.float32) * (place < tiles - 1).astype(jnp.float32)
        parts = ((0, MARGIN, left_w, mleft), (MARGIN, owned - MARGIN, None, None), (owned - MARGIN, owned, right_w, mright))
        for low, high, side_w, side in parts:
            w = own_w[low:high]
            inv = 1.0 / (w if side is None else w + side_w)
            for f in range(GROUP):
                frame = g * GROUP + f
                for r in range(rows):
                    for h in range(channels // LANES):
                        lanes = slice(h * LANES, (h + 1) * LANES)
                        total_term = obuf[frame, r, MARGIN + low : MARGIN + high, lanes].astype(jnp.float32) * w
                        if side is not None:
                            total_term = total_term + side[frame, r, :, lanes].astype(jnp.float32) * side_w
                        bbuf[frame, r, low:high, lanes] = (total_term * inv).astype(jnp.bfloat16)
        give(g).start()

    def step(g):
        at = pl.ds(g * GROUP, GROUP)

        @pl.when(first)
        def _():
            own(g).wait()
            for copy in halos(g):
                copy.wait_recv()

            @pl.when(place == 0)
            def _():
                xbuf[at, :, 0:MARGIN, :] = jnp.zeros((GROUP, rows, MARGIN, channels), jnp.bfloat16)

            @pl.when(place == tiles - 1)
            def _():
                xbuf[at, :, MARGIN + owned : columns, :] = jnp.zeros((GROUP, rows, MARGIN, channels), jnp.bfloat16)

        @pl.when(last)
        def _():
            forward(g).wait_recv()

        hbuf[...] = xbuf[at].astype(jnp.float32)

        if g == 0:
            for copy in loads(0):
                copy.wait()

        hbuf[...] = conv(0, g)

        if g == 0:
            for copy in loads(1):
                copy.wait()

        obuf[at] = (xbuf[at].astype(jnp.float32) + conv(1, g)).astype(jnp.bfloat16)

        @pl.when(first)
        def _():
            forward(g).start()

        @pl.when(last)
        def _():
            for copy in margins(g):
                copy.start()

            if g == 0:
                for copy in weight_sides():
                    copy.wait_recv()
            else:
                blend(g - 1)

    for g in range(groups):
        step(g)

    @pl.when(last)
    def _():
        blend(groups - 1)
        for copy in weight_sides():
            copy.wait_send()
        for g in range(groups):
            for copy in margins(g):
                copy.wait_send()
            if g < half:
                give(g).wait_send()
            else:
                give(g).wait()

    @pl.when(first)
    def _():
        for g in range(groups):
            for copy in halos(g):
                copy.wait_send()
            forward(g).wait_send()
        for g in range(half):
            give(g).wait_recv()


def body(tiles, frames, spatial_weight, temporal_weight, ramp, intersection):
    total, rows, owned, channels = frames.shape
    columns = owned + 2 * MARGIN
    groups = total // GROUP
    bf16, f32 = jnp.bfloat16, jnp.float32
    dma = pltpu.SemaphoreType.DMA
    return pl.pallas_call(
        functools.partial(kernel, tiles),
        out_shape=jax.ShapeDtypeStruct((total // 2, rows, owned, channels), bf16),
        in_specs=[
            pl.BlockSpec(memory_space=pltpu.HBM),
            pl.BlockSpec(memory_space=pltpu.HBM),
            pl.BlockSpec(memory_space=pltpu.HBM),
            pl.BlockSpec(memory_space=pltpu.VMEM),
            pl.BlockSpec(memory_space=pltpu.SMEM),
        ],
        out_specs=pl.BlockSpec(memory_space=pl.ANY),
        scratch_shapes=[
            pltpu.VMEM((total, rows, columns, channels), bf16),
            pltpu.VMEM((total, rows, columns, channels), bf16),
            pltpu.VMEM((2, total + 2, rows, columns, channels), bf16),
            pltpu.VMEM((GROUP, rows, columns, channels), f32),
            pltpu.VMEM((GROUP * columns, rows * 3 * channels), bf16),
            pltpu.VMEM(spatial_weight.shape[1:], bf16),
            pltpu.VMEM(temporal_weight.shape[1:], bf16),
            pltpu.VMEM((columns, LANES), bf16),
            pltpu.VMEM((MARGIN, LANES), bf16),
            pltpu.VMEM((MARGIN, LANES), bf16),
            pltpu.VMEM((total, rows, MARGIN, channels), bf16),
            pltpu.VMEM((total, rows, MARGIN, channels), bf16),
            pltpu.VMEM((total, rows, owned, channels), bf16),
            dma((groups,)),
            dma((4,)),
            dma((2, groups)),
            dma((2, groups)),
            dma((groups,)),
            dma((groups,)),
            dma((2,)),
            dma((2,)),
            dma((2, groups)),
            dma((2, groups)),
            dma((groups,)),
            dma((groups // 2,)),
        ],
        compiler_params=pltpu.CompilerParams(
            collective_id=0, has_side_effects=True, vmem_limit_bytes=56 * 1024 * 1024
        ),
    )(frames, spatial_weight, temporal_weight, ramp, intersection)


def solution(mesh):
    in_specs = (
        P(None, "stream", "tile", None),
        P("segment", None, None, None),
        P("segment", None, None, None),
        P("tile", None),
        P("tile", None),
    )
    out_specs = P("segment", "stream", "tile", None)
    return jax.shard_map(
        functools.partial(body, mesh.shape["tile"]),
        mesh=mesh, in_specs=in_specs, out_specs=out_specs, check_vma=False,
    )
```

```python
import functools

import jax
import jax.numpy as jnp
from jax import lax
from jax.experimental import pallas as pl
from jax.experimental.pallas import tpu as pltpu
from jax.sharding import PartitionSpec as P

MARGIN = 16
LANES = 128
GROUPS = (2, 2, 2, 2)
STARTS = (0, 2, 4, 6)
EPSILON = 1e-6
MESH = pl.DeviceIdType.MESH


def norm_act(hbuf, sbuf, frames):
    _, rows, columns, channels = hbuf.shape
    count = rows * columns
    halves = channels // LANES
    row8 = lax.broadcasted_iota(jnp.int32, (8, LANES), 0)
    lane8 = lax.broadcasted_iota(jnp.int32, (8, LANES), 1)
    means = jnp.zeros((8, LANES), jnp.float32)
    squares = jnp.zeros((8, LANES), jnp.float32)
    for f in range(frames):
        for h in range(halves):
            x = hbuf[f, :, :, h * LANES : (h + 1) * LANES].reshape(count, LANES)
            mean = jnp.sum(x, axis=0, keepdims=True) * (1.0 / count)
            d = x - mean
            square = jnp.sum(d * d, axis=0, keepdims=True)
            here = row8 == f * halves + h
            means = jnp.where(here, mean, means)
            squares = jnp.where(here, square, squares)
    size = float(count)
    for step in (1, 2, 4):
        low = (lane8 & step) == 0
        mean2 = jnp.where(low, pltpu.roll(means, LANES - step, 1), pltpu.roll(means, step, 1))
        square2 = jnp.where(low, pltpu.roll(squares, LANES - step, 1), pltpu.roll(squares, step, 1))
        d = means - mean2
        squares = squares + square2 + d * d * (0.5 * size)
        means = (means + mean2) * 0.5
        size = 2.0 * size
    scale = lax.rsqrt(squares * (1.0 / size) + EPSILON)
    column = lax.broadcasted_iota(jnp.int32, (columns, LANES), 0)
    for f in range(frames):
        for h in range(halves):
            at = f * halves + h
            mean = means[at : at + 1, :]
            inv = scale[at : at + 1, :]
            for r in range(rows):
                y = (hbuf[f, r, :, h * LANES : (h + 1) * LANES] - mean) * inv
                half = 0.5 * y
                a = half * jnp.tanh(half) + half
                before = jnp.where(column == 0, 0.0, pltpu.roll(a, 1, 0))
                after = jnp.where(column == columns - 1, 0.0, pltpu.roll(a, columns - 1, 0))
                for b, piece in enumerate((before, a, after)):
                    lane = (r * 3 + b) * channels + h * LANES
                    sbuf[f * columns : (f + 1) * columns, lane : lane + LANES] = piece.astype(jnp.bfloat16)


def kernel(
    tiles, frames, sw_hbm, tw_hbm, ramp, inter, out,
    xbuf, obuf, spat, hbuf, sbuf, sw, tw, wtile, wleft, wright, mleft, mright, bbuf,
    own_sem, load_sem, halo_send, halo_recv, fwd_send, fwd_recv,
    wt_send, wt_recv, mg_send, mg_recv, ret_send, ret_recv,
):
    seg = lax.axis_index("segment")
    place = lax.axis_index("tile")
    stream = lax.axis_index("stream")
    total, rows, columns, channels = xbuf.shape
    owned = columns - 2 * MARGIN
    groups = len(GROUPS)
    half = STARTS.index(total // 2)
    left = lax.rem(place + tiles - 1, tiles)
    right = lax.rem(place + 1, tiles)
    first, last = seg == 0, seg == 1

    def loads(k):
        return (
            pltpu.make_async_copy(sw_hbm.at[0, k], sw.at[k], load_sem.at[2 * k]),
            pltpu.make_async_copy(tw_hbm.at[0, k], tw.at[k], load_sem.at[2 * k + 1]),
        )

    def own(g):
        at = pl.ds(STARTS[g], GROUPS[g])
        return pltpu.make_async_copy(
            frames.at[at], xbuf.at[at, :, MARGIN : MARGIN + owned, :], own_sem.at[g]
        )

    def remote(src, dst, send, recv, where):
        return pltpu.make_async_remote_copy(
            src_ref=src, dst_ref=dst, send_sem=send, recv_sem=recv, device_id=where, device_id_type=MESH
        )

    def halos(g):
        at = pl.ds(STARTS[g], GROUPS[g])
        return (
            remote(
                frames.at[at, :, owned - MARGIN : owned, :], xbuf.at[at, :, 0:MARGIN, :],
                halo_send.at[0, g], halo_recv.at[0, g], (seg, right, stream),
            ),
            remote(
                frames.at[at, :, 0:MARGIN, :], xbuf.at[at, :, MARGIN + owned : columns, :],
                halo_send.at[1, g], halo_recv.at[1, g], (seg, left, stream),
            ),
        )

    def forward(g):
        at = pl.ds(STARTS[g], GROUPS[g])
        return remote(obuf.at[at], xbuf.at[at], fwd_send.at[g], fwd_recv.at[g], (1 - seg, place, stream))

    def weight_sides():
        return (
            remote(wtile.at[0:MARGIN], wright, wt_send.at[0], wt_recv.at[0], (seg, left, stream)),
            remote(wtile.at[columns - MARGIN : columns], wleft, wt_send.at[1], wt_recv.at[1], (seg, right, stream)),
        )

    def margins(g):
        at = pl.ds(STARTS[g], GROUPS[g])
        return (
            remote(
                obuf.at[at, :, 0:MARGIN, :], mright.at[at],
                mg_send.at[0, g], mg_recv.at[0, g], (seg, left, stream),
            ),
            remote(
                obuf.at[at, :, columns - MARGIN : columns, :], mleft.at[at],
                mg_send.at[1, g], mg_recv.at[1, g], (seg, right, stream),
            ),
        )

    def give(g):
        at = pl.ds(STARTS[g] % (total // 2), GROUPS[g])
        src = bbuf.at[pl.ds(STARTS[g], GROUPS[g])]
        if g < half:
            return remote(src, out.at[at], ret_send.at[g], ret_recv.at[g], (1 - seg, place, stream))
        return pltpu.make_async_copy(src, out.at[at], ret_send.at[g])

    barrier = pltpu.get_barrier_semaphore()
    for where in ((seg, left, stream), (seg, right, stream), (1 - seg, place, stream)):
        pl.semaphore_signal(barrier, inc=1, device_id=where, device_id_type=MESH)

    @pl.when(first)
    def _():
        own(0).start()

    for copy in loads(0):
        copy.start()

    @pl.when(first)
    def _():
        for g in range(1, groups):
            own(g).start()

    for copy in loads(1):
        copy.start()

    pl.semaphore_wait(barrier, 3)

    @pl.when(first)
    def _():
        for g in range(groups):
            for copy in halos(g):
                copy.start()

    @pl.when(last)
    def _():
        eye = lax.broadcasted_iota(jnp.int32, (columns, columns), 0) == lax.broadcasted_iota(
            jnp.int32, (columns, columns), 1
        )
        spread = jnp.where(eye, ramp[...].astype(jnp.float32), 0.0)
        weight = jnp.broadcast_to(jnp.sum(spread, axis=1, keepdims=True), (columns, LANES))
        position = lax.broadcasted_iota(jnp.int32, (columns, LANES), 0)
        inside = (position >= MARGIN - inter[0, 0]) & (position < MARGIN + owned + inter[0, 1])
        wtile[...] = jnp.where(inside, weight, 0.0).astype(jnp.bfloat16)
        for copy in weight_sides():
            copy.start()

    for k in range(2):
        spat[k, 0:2] = jnp.zeros((2, rows, columns, channels), jnp.bfloat16)

    def conv(k, g):
        size, start = GROUPS[g], STARTS[g]
        norm_act(hbuf, sbuf, size)
        taps = 2 * 3 * channels
        act = sbuf[0 : size * columns]
        for r in range(rows):
            low = (1 - r) * 3 * channels
            product = jnp.dot(act, sw[k, low : low + taps, :], preferred_element_type=jnp.float32)
            spat[k, start + 2 : start + 2 + size, r] = product.reshape(size, columns, channels).astype(jnp.bfloat16)
        pieces = [
            spat[k, start + q : start + q + size].reshape(size * rows * columns, channels) for q in range(3)
        ]
        product = jnp.dot(jnp.concatenate(pieces, axis=-1), tw[k], preferred_element_type=jnp.float32)
        return product.reshape(size, rows, columns, channels)

    def blend(g):
        for copy in margins(g):
            copy.wait_recv()
        own_w = wtile[MARGIN : MARGIN + owned, :].astype(jnp.float32)
        left_w = wleft[...].astype(jnp.float32) * (place > 0).astype(jnp.float32)
        right_w = wright[...].astype(jnp.float32) * (place < tiles - 1).astype(jnp.float32)
        parts = ((0, MARGIN, left_w, mleft), (MARGIN, owned - MARGIN, None, None), (owned - MARGIN, owned, right_w, mright))
        for low, high, side_w, side in parts:
            w = own_w[low:high]
            inv = 1.0 / (w if side is None else w + side_w)
            for frame in range(STARTS[g], STARTS[g] + GROUPS[g]):
                for r in range(rows):
                    for h in range(channels // LANES):
                        lanes = slice(h * LANES, (h + 1) * LANES)
                        total_term = obuf[frame, r, MARGIN + low : MARGIN + high, lanes].astype(jnp.float32) * w
                        if side is not None:
                            total_term = total_term + side[frame, r, :, lanes].astype(jnp.float32) * side_w
                        bbuf[frame, r, low:high, lanes] = (total_term * inv).astype(jnp.bfloat16)
        give(g).start()

    def step(g):
        at = pl.ds(STARTS[g], GROUPS[g])

        @pl.when(first)
        def _():
            own(g).wait()
            for copy in halos(g):
                copy.wait_recv()

            @pl.when(place == 0)
            def _():
                xbuf[at, :, 0:MARGIN, :] = jnp.zeros((GROUPS[g], rows, MARGIN, channels), jnp.bfloat16)

            @pl.when(place == tiles - 1)
            def _():
                xbuf[at, :, MARGIN + owned : columns, :] = jnp.zeros((GROUPS[g], rows, MARGIN, channels), jnp.bfloat16)

        @pl.when(last)
        def _():
            forward(g).wait_recv()

        hbuf[0 : GROUPS[g]] = xbuf[at].astype(jnp.float32)

        if g == 0:
            for copy in loads(0):
                copy.wait()

        hbuf[0 : GROUPS[g]] = conv(0, g)

        if g == 0:
            for copy in loads(1):
                copy.wait()

        obuf[at] = (xbuf[at].astype(jnp.float32) + conv(1, g)).astype(jnp.bfloat16)

        @pl.when(first)
        def _():
            forward(g).start()

        @pl.when(last)
        def _():
            for copy in margins(g):
                copy.start()

            if g == 0:
                for copy in weight_sides():
                    copy.wait_recv()
            else:
                blend(g - 1)

    for g in range(groups):
        step(g)

    @pl.when(last)
    def _():
        blend(groups - 1)
        for copy in weight_sides():
            copy.wait_send()
        for g in range(groups):
            for copy in margins(g):
                copy.wait_send()
            if g < half:
                give(g).wait_send()
            else:
                give(g).wait()

    @pl.when(first)
    def _():
        for g in range(groups):
            for copy in halos(g):
                copy.wait_send()
            forward(g).wait_send()
        for g in range(half):
            give(g).wait_recv()


def body(tiles, frames, spatial_weight, temporal_weight, ramp, intersection):
    total, rows, owned, channels = frames.shape
    columns = owned + 2 * MARGIN
    groups = len(GROUPS)
    bf16, f32 = jnp.bfloat16, jnp.float32
    dma = pltpu.SemaphoreType.DMA
    return pl.pallas_call(
        functools.partial(kernel, tiles),
        out_shape=pltpu.VMEM((total // 2, rows, owned, channels), bf16),
        in_specs=[
            pl.BlockSpec(memory_space=pltpu.HBM),
            pl.BlockSpec(memory_space=pltpu.HBM),
            pl.BlockSpec(memory_space=pltpu.HBM),
            pl.BlockSpec(memory_space=pltpu.VMEM),
            pl.BlockSpec(memory_space=pltpu.SMEM),
        ],
        out_specs=pl.BlockSpec(memory_space=pl.ANY),
        scratch_shapes=[
            pltpu.VMEM((total, rows, columns, channels), bf16),
            pltpu.VMEM((total, rows, columns, channels), bf16),
            pltpu.VMEM((2, total + 2, rows, columns, channels), bf16),
            pltpu.VMEM((max(GROUPS), rows, columns, channels), f32),
            pltpu.VMEM((max(GROUPS) * columns, rows * 3 * channels), bf16),
            pltpu.VMEM(spatial_weight.shape[1:], bf16),
            pltpu.VMEM(temporal_weight.shape[1:], bf16),
            pltpu.VMEM((columns, LANES), bf16),
            pltpu.VMEM((MARGIN, LANES), bf16),
            pltpu.VMEM((MARGIN, LANES), bf16),
            pltpu.VMEM((total, rows, MARGIN, channels), bf16),
            pltpu.VMEM((total, rows, MARGIN, channels), bf16),
            pltpu.VMEM((total, rows, owned, channels), bf16),
            dma((groups,)),
            dma((4,)),
            dma((2, groups)),
            dma((2, groups)),
            dma((groups,)),
            dma((groups,)),
            dma((2,)),
            dma((2,)),
            dma((2, groups)),
            dma((2, groups)),
            dma((groups,)),
            dma((STARTS.index(total // 2),)),
        ],
        compiler_params=pltpu.CompilerParams(
            collective_id=0, has_side_effects=True, vmem_limit_bytes=56 * 1024 * 1024
        ),
    )(frames, spatial_weight, temporal_weight, ramp, intersection)


def solution(mesh):
    in_specs = (
        P(None, "stream", "tile", None),
        P("segment", None, None, None),
        P("segment", None, None, None),
        P("tile", None),
        P("tile", None),
    )
    out_specs = P("segment", "stream", "tile", None)
    return jax.shard_map(
        functools.partial(body, mesh.shape["tile"]),
        mesh=mesh, in_specs=in_specs, out_specs=out_specs, check_vma=False,
    )
```

```python
import functools

import jax
import jax.numpy as jnp
from jax import lax
from jax.experimental import pallas as pl
from jax.experimental.pallas import tpu as pltpu
from jax.sharding import PartitionSpec as P

MARGIN = 16
LANES = 128
GROUPS = (2, 2, 2, 2)
STARTS = (0, 2, 4, 6)
EPSILON = 1e-6
MESH = pl.DeviceIdType.MESH


def norm_act(hbuf, sbuf, frames):
    _, rows, columns, channels = hbuf.shape
    count = rows * columns
    halves = channels // LANES
    row8 = lax.broadcasted_iota(jnp.int32, (8, LANES), 0)
    lane8 = lax.broadcasted_iota(jnp.int32, (8, LANES), 1)
    means = jnp.zeros((8, LANES), jnp.float32)
    squares = jnp.zeros((8, LANES), jnp.float32)
    for f in range(frames):
        for h in range(halves):
            x = hbuf[f, :, :, h * LANES : (h + 1) * LANES].reshape(count, LANES)
            mean = jnp.sum(x, axis=0, keepdims=True) * (1.0 / count)
            d = x - mean
            square = jnp.sum(d * d, axis=0, keepdims=True)
            here = row8 == f * halves + h
            means = jnp.where(here, mean, means)
            squares = jnp.where(here, square, squares)
    size = float(count)
    for step in (1, 2, 4):
        low = (lane8 & step) == 0
        mean2 = jnp.where(low, pltpu.roll(means, LANES - step, 1), pltpu.roll(means, step, 1))
        square2 = jnp.where(low, pltpu.roll(squares, LANES - step, 1), pltpu.roll(squares, step, 1))
        d = means - mean2
        squares = squares + square2 + d * d * (0.5 * size)
        means = (means + mean2) * 0.5
        size = 2.0 * size
    scale = lax.rsqrt(squares * (1.0 / size) + EPSILON)
    column = lax.broadcasted_iota(jnp.int32, (columns, LANES), 0)
    for f in range(frames):
        for h in range(halves):
            at = f * halves + h
            mean = means[at : at + 1, :]
            inv = scale[at : at + 1, :]
            for r in range(rows):
                y = (hbuf[f, r, :, h * LANES : (h + 1) * LANES] - mean) * inv
                half = 0.5 * y
                a = half * jnp.tanh(half) + half
                before = jnp.where(column == 0, 0.0, pltpu.roll(a, 1, 0))
                after = jnp.where(column == columns - 1, 0.0, pltpu.roll(a, columns - 1, 0))
                for b, piece in enumerate((before, a, after)):
                    lane = (r * 3 + b) * channels + h * LANES
                    sbuf[f * columns : (f + 1) * columns, lane : lane + LANES] = piece.astype(jnp.bfloat16)


def kernel(
    tiles, frames, sw_hbm, tw_hbm, ramp, inter, out,
    xbuf, obuf, spat, hbuf, sbuf, sw, tw, wtile, wleft, wright, mleft, mright, bbuf,
    own_sem, load_sem, halo_send, halo_recv, fwd_send, fwd_recv,
    wt_send, wt_recv, mg_send, mg_recv, ret_send, ret_recv,
):
    seg = lax.axis_index("segment")
    place = lax.axis_index("tile")
    stream = lax.axis_index("stream")
    total, rows, columns, channels = xbuf.shape
    owned = columns - 2 * MARGIN
    groups = len(GROUPS)
    half = STARTS.index(total // 2)
    left = lax.rem(place + tiles - 1, tiles)
    right = lax.rem(place + 1, tiles)
    first, last = seg == 0, seg == 1

    def loads(k):
        return (
            pltpu.make_async_copy(sw_hbm.at[0, k], sw.at[k], load_sem.at[2 * k]),
            pltpu.make_async_copy(tw_hbm.at[0, k], tw.at[k], load_sem.at[2 * k + 1]),
        )

    def own(g):
        at = pl.ds(STARTS[g], GROUPS[g])
        return pltpu.make_async_copy(
            frames.at[at], xbuf.at[at, :, MARGIN : MARGIN + owned, :], own_sem.at[g]
        )

    def remote(src, dst, send, recv, where):
        return pltpu.make_async_remote_copy(
            src_ref=src, dst_ref=dst, send_sem=send, recv_sem=recv, device_id=where, device_id_type=MESH
        )

    def halos(g):
        at = pl.ds(STARTS[g], GROUPS[g])
        return (
            remote(
                frames.at[at, :, owned - MARGIN : owned, :], xbuf.at[at, :, 0:MARGIN, :],
                halo_send.at[0, g], halo_recv.at[0, g], (seg, right, stream),
            ),
            remote(
                frames.at[at, :, 0:MARGIN, :], xbuf.at[at, :, MARGIN + owned : columns, :],
                halo_send.at[1, g], halo_recv.at[1, g], (seg, left, stream),
            ),
        )

    def forward(g):
        at = pl.ds(STARTS[g], GROUPS[g])
        return remote(obuf.at[at], xbuf.at[at], fwd_send.at[g], fwd_recv.at[g], (1 - seg, place, stream))

    def weight_sides():
        return (
            remote(wtile.at[0:MARGIN], wright, wt_send.at[0], wt_recv.at[0], (seg, left, stream)),
            remote(wtile.at[columns - MARGIN : columns], wleft, wt_send.at[1], wt_recv.at[1], (seg, right, stream)),
        )

    def margins(g):
        at = pl.ds(STARTS[g], GROUPS[g])
        return (
            remote(
                obuf.at[at, :, 0:MARGIN, :], mright.at[at],
                mg_send.at[0, g], mg_recv.at[0, g], (seg, left, stream),
            ),
            remote(
                obuf.at[at, :, columns - MARGIN : columns, :], mleft.at[at],
                mg_send.at[1, g], mg_recv.at[1, g], (seg, right, stream),
            ),
        )

    def give(g):
        at = pl.ds(STARTS[g], GROUPS[g])
        return remote(bbuf.at[at], out.at[at], ret_send.at[g], ret_recv.at[g], (1 - seg, place, stream))

    barrier = pltpu.get_barrier_semaphore()
    for where in ((seg, left, stream), (seg, right, stream), (1 - seg, place, stream)):
        pl.semaphore_signal(barrier, inc=1, device_id=where, device_id_type=MESH)

    @pl.when(first)
    def _():
        own(0).start()

    for copy in loads(0):
        copy.start()

    @pl.when(first)
    def _():
        for g in range(1, groups):
            own(g).start()

    for copy in loads(1):
        copy.start()

    pl.semaphore_wait(barrier, 3)

    @pl.when(first)
    def _():
        for g in range(groups):
            for copy in halos(g):
                copy.start()

    @pl.when(last)
    def _():
        eye = lax.broadcasted_iota(jnp.int32, (columns, columns), 0) == lax.broadcasted_iota(
            jnp.int32, (columns, columns), 1
        )
        spread = jnp.where(eye, ramp[...].astype(jnp.float32), 0.0)
        weight = jnp.broadcast_to(jnp.sum(spread, axis=1, keepdims=True), (columns, LANES))
        position = lax.broadcasted_iota(jnp.int32, (columns, LANES), 0)
        inside = (position >= MARGIN - inter[0, 0]) & (position < MARGIN + owned + inter[0, 1])
        wtile[...] = jnp.where(inside, weight, 0.0).astype(jnp.bfloat16)
        for copy in weight_sides():
            copy.start()

    for k in range(2):
        spat[k, 0:2] = jnp.zeros((2, rows, columns, channels), jnp.bfloat16)

    def conv(k, g):
        size, start = GROUPS[g], STARTS[g]
        norm_act(hbuf, sbuf, size)
        taps = 2 * 3 * channels
        act = sbuf[0 : size * columns]
        for r in range(rows):
            low = (1 - r) * 3 * channels
            product = jnp.dot(act, sw[k, low : low + taps, :], preferred_element_type=jnp.float32)
            spat[k, start + 2 : start + 2 + size, r] = product.reshape(size, columns, channels).astype(jnp.bfloat16)
        pieces = [
            spat[k, start + q : start + q + size].reshape(size * rows * columns, channels) for q in range(3)
        ]
        product = jnp.dot(jnp.concatenate(pieces, axis=-1), tw[k], preferred_element_type=jnp.float32)
        return product.reshape(size, rows, columns, channels)

    def blend(g):
        for copy in margins(g):
            copy.wait_recv()
        own_w = wtile[MARGIN : MARGIN + owned, :].astype(jnp.float32)
        left_w = wleft[...].astype(jnp.float32) * (place > 0).astype(jnp.float32)
        right_w = wright[...].astype(jnp.float32) * (place < tiles - 1).astype(jnp.float32)
        parts = ((0, MARGIN, left_w, mleft), (MARGIN, owned - MARGIN, None, None), (owned - MARGIN, owned, right_w, mright))
        for low, high, side_w, side in parts:
            w = own_w[low:high]
            inv = 1.0 / (w if side is None else w + side_w)
            for frame in range(STARTS[g], STARTS[g] + GROUPS[g]):
                for r in range(rows):
                    for h in range(channels // LANES):
                        lanes = slice(h * LANES, (h + 1) * LANES)
                        total_term = obuf[frame, r, MARGIN + low : MARGIN + high, lanes].astype(jnp.float32) * w
                        if side is not None:
                            total_term = total_term + side[frame, r, :, lanes].astype(jnp.float32) * side_w
                        target, row = (bbuf, frame) if g < half else (out, frame - total // 2)
                        target[row, r, low:high, lanes] = (total_term * inv).astype(jnp.bfloat16)
        if g < half:
            give(g).start()

    def step(g):
        at = pl.ds(STARTS[g], GROUPS[g])

        @pl.when(first)
        def _():
            own(g).wait()
            for copy in halos(g):
                copy.wait_recv()

            @pl.when(place == 0)
            def _():
                xbuf[at, :, 0:MARGIN, :] = jnp.zeros((GROUPS[g], rows, MARGIN, channels), jnp.bfloat16)

            @pl.when(place == tiles - 1)
            def _():
                xbuf[at, :, MARGIN + owned : columns, :] = jnp.zeros((GROUPS[g], rows, MARGIN, channels), jnp.bfloat16)

        @pl.when(last)
        def _():
            forward(g).wait_recv()

        hbuf[0 : GROUPS[g]] = xbuf[at].astype(jnp.float32)

        if g == 0:
            for copy in loads(0):
                copy.wait()

        hbuf[0 : GROUPS[g]] = conv(0, g)

        if g == 0:
            for copy in loads(1):
                copy.wait()

        obuf[at] = (xbuf[at].astype(jnp.float32) + conv(1, g)).astype(jnp.bfloat16)

        @pl.when(first)
        def _():
            forward(g).start()

        @pl.when(last)
        def _():
            for copy in margins(g):
                copy.start()

            if g == 0:
                for copy in weight_sides():
                    copy.wait_recv()
            else:
                blend(g - 1)

    for g in range(groups):
        step(g)

    @pl.when(last)
    def _():
        blend(groups - 1)
        for copy in weight_sides():
            copy.wait_send()
        for g in range(groups):
            for copy in margins(g):
                copy.wait_send()
            if g < half:
                give(g).wait_send()

    @pl.when(first)
    def _():
        for g in range(groups):
            for copy in halos(g):
                copy.wait_send()
            forward(g).wait_send()
        for g in range(half):
            give(g).wait_recv()


def body(tiles, frames, spatial_weight, temporal_weight, ramp, intersection):
    total, rows, owned, channels = frames.shape
    columns = owned + 2 * MARGIN
    groups = len(GROUPS)
    bf16, f32 = jnp.bfloat16, jnp.float32
    dma = pltpu.SemaphoreType.DMA
    return pl.pallas_call(
        functools.partial(kernel, tiles),
        out_shape=pltpu.VMEM((total // 2, rows, owned, channels), bf16),
        in_specs=[
            pl.BlockSpec(memory_space=pltpu.HBM),
            pl.BlockSpec(memory_space=pltpu.HBM),
            pl.BlockSpec(memory_space=pltpu.HBM),
            pl.BlockSpec(memory_space=pltpu.VMEM),
            pl.BlockSpec(memory_space=pltpu.SMEM),
        ],
        out_specs=pl.BlockSpec(memory_space=pltpu.VMEM),
        scratch_shapes=[
            pltpu.VMEM((total, rows, columns, channels), bf16),
            pltpu.VMEM((total, rows, columns, channels), bf16),
            pltpu.VMEM((2, total + 2, rows, columns, channels), bf16),
            pltpu.VMEM((max(GROUPS), rows, columns, channels), f32),
            pltpu.VMEM((max(GROUPS) * columns, rows * 3 * channels), bf16),
            pltpu.VMEM(spatial_weight.shape[1:], bf16),
            pltpu.VMEM(temporal_weight.shape[1:], bf16),
            pltpu.VMEM((columns, LANES), bf16),
            pltpu.VMEM((MARGIN, LANES), bf16),
            pltpu.VMEM((MARGIN, LANES), bf16),
            pltpu.VMEM((total, rows, MARGIN, channels), bf16),
            pltpu.VMEM((total, rows, MARGIN, channels), bf16),
            pltpu.VMEM((total // 2, rows, owned, channels), bf16),
            dma((groups,)),
            dma((4,)),
            dma((2, groups)),
            dma((2, groups)),
            dma((groups,)),
            dma((groups,)),
            dma((2,)),
            dma((2,)),
            dma((2, groups)),
            dma((2, groups)),
            dma((groups,)),
            dma((STARTS.index(total // 2),)),
        ],
        compiler_params=pltpu.CompilerParams(
            collective_id=0, has_side_effects=True, vmem_limit_bytes=56 * 1024 * 1024
        ),
    )(frames, spatial_weight, temporal_weight, ramp, intersection)


def solution(mesh):
    in_specs = (
        P(None, "stream", "tile", None),
        P("segment", None, None, None),
        P("segment", None, None, None),
        P("tile", None),
        P("tile", None),
    )
    out_specs = P("segment", "stream", "tile", None)
    return jax.shard_map(
        functools.partial(body, mesh.shape["tile"]),
        mesh=mesh, in_specs=in_specs, out_specs=out_specs, check_vma=False,
    )
```
